32 devices in a mesh: dp: 4 (over x, core), ctx: 8 (over z, y).
Axes of the slice: x: 2, y: 2, z: 4, core: 2. Of those that a mesh axis runs over, the one named last changes fastest.
Arguments:
- tokens: bfloat16 [4, 1024, 1536], P('dp', 'ctx'), may hold values from -6 to 6
- positions: int32 [4, 1024], P('dp', 'ctx'), may hold values from 0 to 255, as said below
- segments: int32 [4, 1024], P('dp', 'ctx'), may hold values from 0 to 7, as said below
- qkv_weight: bfloat16 [1536, 2048], P(('dp', 'ctx')), may hold values from -0.15625 to 0.15625
- qkv_bias: bfloat16 [2048], P(('dp', 'ctx')), may hold values from -3 to 3
- out_weight: bfloat16 [1536, 1536], P(('dp', 'ctx')), may hold values from -1.25 to 1.25
- norm_one: bfloat16 [1536], P(('dp', 'ctx')), may hold values from 0.099609375 to 1.8984375
- norm_two: bfloat16 [1536], P(('dp', 'ctx')), may hold values from 0.099609375 to 1.8984375
- gate_up: bfloat16 [8960, 2, 1536], P(('dp', 'ctx')), may hold values from -0.15625 to 0.15625
- down_weight: bfloat16 [8960, 1536], P(('dp', 'ctx')), may hold values from -0.0625 to 0.0625
- cotangent: bfloat16 [4, 1024, 1536], P('dp', 'ctx'), may hold values from -6 to 6
Outputs:
- output: bfloat16 [4, 1024, 1536], P('dp', 'ctx')
- input_grad: bfloat16 [4, 1024, 1536], P('dp', 'ctx')
- qkv_weight_grad: float32 [1536, 2048], P(('dp', 'ctx'))
- qkv_bias_grad: float32 [2048], P(('dp', 'ctx'))
- out_weight_grad: float32 [1536, 1536], P(('dp', 'ctx'))
- norm_one_grad: float32 [1536], P(('dp', 'ctx'))
- norm_two_grad: float32 [1536], P(('dp', 'ctx'))
- gate_up_grad: float32 [8960, 2, 1536], P(('dp', 'ctx'))
- down_weight_grad: float32 [8960, 1536], P(('dp', 'ctx'))
The draws below stay inside these ranges and needn't reach their ends.
Inputs may be any that keep to these rules, and one draw needn't show every extreme that they name: `segments`: documents are contiguous runs of a sequence, numbered from 0 in order; each sequence holds 8 of them and one has exactly 256 tokens, none more. `positions`: counts from 0 at each document's first token.
All inputs are finite; a program needn't handle non-finite values.
Results may differ from the reference program's by a relative error of at most 0.014.
Values may be sent and summed in bfloat16 or wider, within the bound.
No kernel may reach another device: no remote copies, remote signals or barrier semaphores. Data moves between devices by JAX's collectives and lax.ppermute only.
A program may use at most 448 MiB of HBM per device.

```python
import math
import jax
import jax.numpy as jnp
from jax import lax

D = 1536
HEADS = 12
KV_HEADS = 2
HEAD = 128
FF = 8960
QD = 1536
KVD = 256
SEQ = 1024
SEQS = 4
DOC_MOST = 256
DOCS = 8


def document_row(row_key):
    longest = DOC_MOST
    count_docs = DOCS
    others = count_docs - 1
    remainder = SEQ - longest
    spread = remainder // (4 * others)
    key_cut, key_place = jax.random.split(row_key)
    inner_cuts = jnp.arange(1, others, dtype=jnp.int32)
    jitter = jax.random.randint(key_cut, (others - 1,), -spread, spread + 1).astype(jnp.int32)
    cut_points = inner_cuts * remainder // others + jitter
    boundaries = jnp.concatenate([jnp.zeros((1,), jnp.int32), cut_points, jnp.full((1,), remainder, jnp.int32)])
    other_lengths = boundaries[1:] - boundaries[:-1]
    long_slot = jax.random.randint(key_place, (), 0, count_docs).astype(jnp.int32)
    doc_index = jnp.arange(count_docs, dtype=jnp.int32)
    before = other_lengths[jnp.minimum(doc_index, others - 1)]
    shifted = other_lengths[jnp.maximum(doc_index - 1, 0)]
    lengths = jnp.where(doc_index < long_slot, before, jnp.where(doc_index == long_slot, longest, shifted)).astype(jnp.int32)
    starts = jnp.cumsum(lengths) - lengths
    places = jnp.arange(SEQ, dtype=jnp.int32)
    doc_ids = jnp.sum((starts[None, 1:] <= places[:, None]).astype(jnp.int32), axis=1)
    doc_start = jnp.sum(jnp.where(doc_ids[:, None] == doc_index[None, :], starts[None, :], 0), axis=1)
    return (doc_ids.astype(jnp.int32), (places - doc_start).astype(jnp.int32))


def document_tables(key):
    base_key = jax.random.fold_in(key, 11)
    row_ids = jnp.arange(SEQS)
    return jax.vmap(lambda row_id: document_row(jax.random.fold_in(base_key, row_id)))(row_ids)


def draw_segments(key, part):
    return document_tables(key)[0]


def draw_positions(key, part):
    return document_tables(key)[1]


def with_spikes(entries, stream_key, source, target, parts, factor):
    def block_of(axis_at):
        return (jnp.arange(entries.shape[axis_at]) // (entries.shape[axis_at] // parts)).reshape((-1,) + (1,) * (entries.ndim - 1 - axis_at))

    first = jax.random.permutation(stream_key, parts)[block_of(target)]
    other_side = (block_of(target) + parts // 2) % parts
    return jnp.where((block_of(source) == first) | (block_of(source) == other_side), factor * entries, entries)


def block_levels(rng, dims, cuts, least, largest):
    loudness, own = 1.0, jax.random.fold_in(rng, 6)
    for axis_at, shards_of in cuts:
        draws = jnp.exp(jax.random.uniform(jax.random.fold_in(own, axis_at), (shards_of,), jnp.float32, least / len(cuts), largest / len(cuts)))
        loudness = loudness * jnp.repeat(draws, dims[axis_at] // shards_of).reshape([-1 if axis == axis_at else 1 for axis in range(len(dims))])
    return loudness


def scatter_about(rng, extent, deviation, bound, shards=(), kind=jnp.bfloat16):
    drawn = jax.random.normal(rng, extent, jnp.float32) * deviation
    if len(shards) > 0:
        drawn = block_levels(rng, extent, shards, -0.22, 0.18) * drawn
    return jnp.clip(drawn, min=-bound, max=bound).astype(kind)


def heavy_noise(rng, shape, scale, reach, shards, heavy, kind=jnp.bfloat16):
    values = scale * jax.random.normal(rng, shape, jnp.float32)
    if shards:
        values = values * block_levels(rng, shape, shards, -0.22, 0.18)
    return jnp.clip(with_spikes(values, jax.random.fold_in(rng, 3), *heavy), -reach, reach).astype(kind)


def setup_inputs(seed: int = 0) -> dict:
    splits = jax.random.split(jax.random.key(seed), 12)
    return {
        "tokens": scatter_about(splits[0], (SEQS, SEQ, D), 1.0, 6.0, ((0, 4), (1, 8))),
        "positions": draw_positions(jax.random.fold_in(splits[11], 71), 0),
        "segments": draw_segments(jax.random.fold_in(splits[11], 71), 0),
        "qkv_weight": scatter_about(splits[3], (D, QD + 2 * KVD), D ** -0.5, 0.15625, ((0, 32),)),
        "qkv_bias": scatter_about(splits[4], (QD + 2 * KVD,), 0.5, 3.0, ((0, 32),)),
        "out_weight": scatter_about(splits[5], (QD, D), (QD // 64) ** -0.5, 1.25, ((0, 32),)),
        "norm_one": jnp.clip(1.0 + 0.18 * jax.random.normal(splits[6], (D,), jnp.float32), 0.099609375, 1.8984375).astype(jnp.bfloat16),
        "norm_two": jnp.clip(1.0 + 0.18 * jax.random.normal(splits[7], (D,), jnp.float32), 0.099609375, 1.8984375).astype(jnp.bfloat16),
        "gate_up": scatter_about(splits[8], (FF, 2, D), D ** -0.5, 0.15625, ((0, 32),)),
        "down_weight": scatter_about(splits[9], (FF, D), FF ** -0.5, 0.0625, ((0, 32),)),
        "cotangent": heavy_noise(splits[10], (SEQS, SEQ, D), 1.0, 6.0, ((0, 4), (1, 8)), (1, 2, 8, 2.0)),
    }


EPSILON = 1e-06
ROPE_BASE = 1000000.0
PRECISE = lax.Precision.HIGHEST

@jax.custom_vjp
def low(v):
    return lax.optimization_barrier(v.astype(jnp.bfloat16)).astype(jnp.float32)

@jax.custom_vjp
def low_back(v):
    return v

def low_keep(v):
    return (low(v), None)

def low_pass(kept, grad):
    return (grad,)

def back_keep(v):
    return (v, None)

def back_low(kept, grad):
    return (low(grad),)
low.defvjp(low_keep, low_pass)
low_back.defvjp(back_keep, back_low)

def rope_tables(seq_positions):
    half_width = HEAD // 2
    exponents = jnp.arange(half_width, dtype=jnp.float32) * (2.0 / HEAD)
    frequency = jnp.power(jnp.float32(ROPE_BASE), -exponents)
    angles = seq_positions.astype(jnp.float32)[:, None] * frequency[None, :]
    return (jnp.cos(angles), jnp.sin(angles))

def rotate(values, cosine, sine_vals):
    half_width = values.shape[-1] // 2
    lower_half = values[..., :half_width]
    upper_half = values[..., half_width:]
    cos_wide = cosine[:, None, :]
    sin_wide = sine_vals[:, None, :]
    return jnp.concatenate([lower_half * cos_wide - upper_half * sin_wide, upper_half * cos_wide + lower_half * sin_wide], axis=-1)

def rms_norm(tok_rows, gain_vec):
    row_scale = lax.rsqrt(lax.optimization_barrier(jnp.mean(tok_rows * tok_rows, axis=-1, keepdims=True)) + EPSILON)
    return tok_rows * row_scale * gain_vec

def attention(query_rot, key_rot, value_rot, seq_segments):
    block_rows = min(512, SEQ)
    pad_rows = DOC_MOST
    group_size = HEADS // KV_HEADS
    key_pad = jnp.pad(key_rot, ((pad_rows, 0), (0, 0), (0, 0)))
    value_pad = jnp.pad(value_rot, ((pad_rows, 0), (0, 0), (0, 0)))
    seg_pad = jnp.pad(seq_segments, (pad_rows, 0), constant_values=-1)

    def one_block(first_row):
        query_blk = lax.dynamic_slice_in_dim(query_rot, first_row, block_rows, 0).reshape(block_rows, KV_HEADS, group_size, HEAD)
        key_blk = lax.dynamic_slice_in_dim(key_pad, first_row, block_rows + pad_rows, 0)
        value_blk = lax.dynamic_slice_in_dim(value_pad, first_row, block_rows + pad_rows, 0)
        seg_query = lax.dynamic_slice_in_dim(seq_segments, first_row, block_rows, 0)
        seg_key = lax.dynamic_slice_in_dim(seg_pad, first_row, block_rows + pad_rows, 0)
        query_index = first_row + jnp.arange(block_rows)
        key_index = first_row - pad_rows + jnp.arange(block_rows + pad_rows)
        allowed = (seg_query[:, None] == seg_key[None, :]) & (key_index[None, :] <= query_index[:, None])
        scores = jnp.einsum('qgmd,kgd->gmqk', query_blk, key_blk, precision=PRECISE) * (1.0 / math.sqrt(HEAD))
        scores = low_back(scores)
        scores = jnp.where(allowed, scores, -jnp.inf)
        row_top = lax.optimization_barrier(jnp.max(scores, axis=-1, keepdims=True))
        raised = jnp.exp(scores - row_top)
        prob_vals = low(raised / lax.optimization_barrier(jnp.sum(raised, axis=-1, keepdims=True)))
        attended = jnp.einsum('gmqk,kgd->qgmd', prob_vals, value_blk, precision=PRECISE)
        return attended.reshape(block_rows, HEADS * HEAD)
    block_starts = jnp.arange(SEQ // block_rows, dtype=jnp.int32) * block_rows
    return lax.map(jax.checkpoint(one_block), block_starts).reshape(SEQ, HEADS * HEAD)

def sequence_forward(tok_rows, seq_positions, seq_segments, qkv_weight, qkv_bias, out_weight, norm_one, norm_two, gate_up, down_weight):
    query_width = HEADS * HEAD
    key_width = KV_HEADS * HEAD
    act_one = low(rms_norm(tok_rows, norm_one))
    qkv_all = low_back(jnp.dot(act_one, qkv_weight, precision=PRECISE) + qkv_bias)
    cosine, sine_vals = rope_tables(seq_positions)
    query_rot = low(rotate(qkv_all[:, :query_width].reshape(SEQ, HEADS, HEAD), cosine, sine_vals))
    key_rot = low(rotate(qkv_all[:, query_width:query_width + key_width].reshape(SEQ, KV_HEADS, HEAD), cosine, sine_vals))
    value_rot = low(qkv_all[:, query_width + key_width:].reshape(SEQ, KV_HEADS, HEAD))
    attended = low(low_back(attention(query_rot, key_rot, value_rot, seq_segments)))
    resid_state = tok_rows + low_back(jnp.dot(attended, out_weight, precision=PRECISE))
    act_two = low(rms_norm(resid_state, norm_two))
    row_block = min(2048, SEQ)

    def mlp_block(act_rows):
        gate_val = low_back(jnp.einsum('td,fd->tf', act_rows, gate_up[:, 0], precision=PRECISE))
        up_val = low_back(jnp.einsum('td,fd->tf', act_rows, gate_up[:, 1], precision=PRECISE))
        hidden = low(jax.nn.silu(gate_val) * up_val)
        return jnp.dot(hidden, down_weight, precision=PRECISE)
    mlp_out = lax.map(jax.checkpoint(mlp_block), act_two.reshape(SEQ // row_block, row_block, D)).reshape(SEQ, D)
    return resid_state + low_back(mlp_out)

def reference(tokens, positions, segments, qkv_weight, qkv_bias, out_weight, norm_one, norm_two, gate_up, down_weight, cotangent):
    params = (qkv_weight.astype(jnp.float32), qkv_bias.astype(jnp.float32), out_weight.astype(jnp.float32), norm_one.astype(jnp.float32), norm_two.astype(jnp.float32), gate_up.astype(jnp.float32), down_weight.astype(jnp.float32))

    def one_sequence(totals, inputs):
        seq_tokens, seq_positions, seq_segments, seq_cot = inputs

        def forward(tok_rows, *weights):
            return sequence_forward(tok_rows, seq_positions, seq_segments, *weights)
        result, pullback = jax.vjp(forward, seq_tokens.astype(jnp.float32), *params)
        grads = pullback(seq_cot.astype(jnp.float32))
        totals = jax.tree.map(jnp.add, totals, tuple(grads[1:]))
        return (totals, (result.astype(jnp.bfloat16), grads[0].astype(jnp.bfloat16)))
    zero_grads = tuple((jnp.zeros(param.shape, jnp.float32) for param in params))
    totals, (outputs, input_grads) = lax.scan(one_sequence, zero_grads, (tokens, positions, segments, cotangent))
    return (outputs, input_grads, totals[0], totals[1], totals[2], totals[3], totals[4], totals[5], totals[6])
```

```python
import math

import jax
import jax.numpy as jnp
from jax import lax
from jax.experimental import pallas as pl
from jax.experimental.pallas import tpu as pltpu
from jax.sharding import PartitionSpec as P

HEADS = 12
KV_HEADS = 2
HEAD = 128
DOC_CAP = 2000


EPSILON = 1e-06
ROPE_BASE = 1000000.0


def from_behind(block, distance):
    devices = range(lax.axis_size("ctx"))
    route = [(i - distance, i) for i in devices if i - distance in devices]
    return lax.ppermute(block, "ctx", route)


def ring_of(count):
    return [*range(0, count, 2), *range(count - 1, 0, -2)]


def ahead(block):
    ring = ring_of(lax.axis_size("ctx"))
    return lax.ppermute(block, "ctx", list(zip(ring, ring[1:] + ring[:1])))


def back(block):
    ring = ring_of(lax.axis_size("ctx"))
    return lax.ppermute(block, "ctx", list(zip(ring[1:] + ring[:1], ring)))


def core_swap(block):
    return lax.ppermute(block, "dp", [(i, i ^ 1) for i in range(lax.axis_size("dp"))])


def pair_swap(block):
    return lax.ppermute(block, "dp", [(i, i ^ 2) for i in range(lax.axis_size("dp"))])


def sum_all(values):
    for axis in ("dp", "ctx"):
        size = lax.axis_size(axis)
        bit = 1
        while bit < size:
            values = values + lax.ppermute(values, axis, [(i, i ^ bit) for i in range(size)])
            bit *= 2
    return values


def ring_gather(block, between=None):
    count = lax.axis_size("ctx")
    half = block.shape[0] // 2
    pieces, up, down = [block], block, block
    for _ in range(1, count // 2):
        waits = between(pieces) if between else []
        up, down = ahead(up), back(down)
        pieces += [up, down]
        if waits:
            up, down = after((up, down), *waits)
    return pieces + [ahead(up[:half]), back(down[half:])]


def ring_scatter(parts, between=()):
    count = lax.axis_size("ctx")
    between = list(between)

    def low(part):
        return part.astype(jnp.bfloat16)

    first, second = back(low(parts[-2])), ahead(low(parts[-1]))
    half = parts[-2].shape[0]
    for distance in range(count // 2 - 1, 0, -1):
        lower, upper = parts[2 * distance - 1], parts[2 * distance]
        if distance == count // 2 - 1:
            lower = jnp.concatenate([lower[:half] + first.astype(jnp.float32), lower[half:]])
            upper = jnp.concatenate([upper[:half], upper[half:] + second.astype(jnp.float32)])
        else:
            lower = lower + first.astype(jnp.float32)
            upper = upper + second.astype(jnp.float32)
        lower, upper = low(lower), low(upper)
        if between:
            lower, upper = after((lower, upper), *between.pop(0))
        first, second = back(lower), ahead(upper)
    return parts[0] + (first.astype(jnp.float32) + second.astype(jnp.float32))


def ring_positions():
    count = lax.axis_size("ctx")
    place = lax.axis_index("ctx")
    position = jnp.where(place % 2 == 0, place // 2, count - (place + 1) // 2)
    offsets = [0]
    for distance in range(1, count // 2):
        offsets += [-distance, distance]
    offsets.append(count // 2)
    at = (position + jnp.array(offsets, jnp.int32) + count) % count
    return jnp.where(at < count // 2, 2 * at, 2 * count - 2 * at - 1)


def owner_order():
    count = lax.axis_size("ctx")
    place = lax.axis_index("dp")
    flips = jnp.arange(2, dtype=jnp.int32)
    core = (place % 2) ^ flips
    pair = (place // 2) ^ flips
    owners = (pair[None, None, :] * 2 + core[:, None, None]) * count
    return (owners + ring_positions()[None, :, None]).reshape(-1)


def place_blocks(pieces, order):
    total = sum(piece.shape[0] for piece in pieces)
    tail = pieces[0].shape[1:]

    def body(order_ref, *refs):
        sources, out_ref, sems = refs[:-2], refs[-2], refs[-1]
        copies = []
        for source in sources:
            for inner in range(source.shape[0]):
                index = len(copies)
                copies.append(
                    pltpu.make_async_copy(
                        source.at[inner], out_ref.at[order_ref[index]], sems.at[index]
                    )
                )
        for copy in copies:
            copy.start()
        for copy in copies:
            copy.wait()

    return pl.pallas_call(
        body,
        out_shape=jax.ShapeDtypeStruct((total, *tail), pieces[0].dtype),
        in_specs=[pl.BlockSpec(memory_space=pltpu.SMEM)]
        + [pl.BlockSpec(memory_space=pl.ANY)] * len(pieces),
        out_specs=pl.BlockSpec(memory_space=pltpu.VMEM),
        scratch_shapes=[pltpu.SemaphoreType.DMA((total,))],
        name="place_blocks",
    )(order, *pieces)


def pick_blocks(blocks, order):
    def body(order_ref, in_ref, out_ref):
        for index in range(blocks.shape[0]):
            out_ref[index] = in_ref[order_ref[index]]

    return pl.pallas_call(
        body,
        out_shape=jax.ShapeDtypeStruct(blocks.shape, blocks.dtype),
        in_specs=[
            pl.BlockSpec(memory_space=pltpu.SMEM),
            pl.BlockSpec(memory_space=pltpu.VMEM),
        ],
        out_specs=pl.BlockSpec(memory_space=pltpu.VMEM),
        name="pick_blocks",
    )(order, blocks)


def gather_rows(both, order):
    mine = ring_gather(both)
    theirs = [core_swap(piece) for piece in mine]
    whole = place_blocks(mine + theirs, order)
    return whole.reshape(-1, both.shape[2]), mine[-1]


def scatter_rows(columns, rows, order):
    count = lax.axis_size("ctx")
    owners = order.shape[0]
    turned = jnp.transpose(columns).reshape(owners, -1, columns.shape[0])
    turned = pick_blocks(turned, order).reshape(columns.shape[1], columns.shape[0])
    half = columns.shape[1] // 2
    theirs = contract(turned[half:], rows, 1, 0).astype(jnp.bfloat16)
    received = core_swap(theirs)
    mine = contract(turned[:half], rows, 1, 0) + received.astype(jnp.float32)
    mine = mine.reshape(count, 2, -1, rows.shape[1])
    parts = [mine[i] for i in range(count - 1)] + [mine[count - 1, :1], mine[count - 1, 1:]]
    own = ring_scatter(parts)
    return own[0] + pair_swap(own[1].astype(jnp.bfloat16)).astype(jnp.float32)


def contract(lhs_array, rhs_array, lhs_dim, rhs_dim):
    return lax.dot_general(
        lhs_array,
        rhs_array,
        (((lhs_dim,), (rhs_dim,)), ((), ())),
        preferred_element_type=jnp.float32,
    )


def rope_tables(seq_positions):
    half_width = HEAD // 2
    exponents = jnp.arange(half_width, dtype=jnp.float32) * (2.0 / HEAD)
    frequency = jnp.power(jnp.float32(ROPE_BASE), -exponents)
    angles = seq_positions.astype(jnp.float32)[:, None] * frequency[None, :]
    return (jnp.cos(angles), jnp.sin(angles))


def rotate(values, cosine, sine_vals):
    half_width = values.shape[-1] // 2
    lower_half = values[..., :half_width]
    upper_half = values[..., half_width:]
    cos_wide = cosine[:, None, :]
    sin_wide = sine_vals[:, None, :]
    return jnp.concatenate(
        [
            lower_half * cos_wide - upper_half * sin_wide,
            upper_half * cos_wide + lower_half * sin_wide,
        ],
        axis=-1,
    )


def unrotate(grads, cosine, sine_vals):
    return rotate(grads, cosine, -sine_vals)


def rms_back(grad_act, normed, row_scale, gain_vec):
    grad_normed = grad_act * gain_vec
    return row_scale * (
        grad_normed - normed * jnp.mean(grad_normed * normed, axis=-1, keepdims=True)
    )


def after(value, *others):
    return lax.optimization_barrier((value, *others))[0]


def shards(
    tokens,
    positions,
    segments,
    qkv_weight,
    qkv_bias,
    out_weight,
    norm_one,
    norm_two,
    gate_up,
    down_weight,
    cotangent,
):
    tok_rows = tokens[0].astype(jnp.float32)
    length, width = tok_rows.shape
    query_width = HEADS * HEAD
    key_width = KV_HEADS * HEAD
    head_group = HEADS // KV_HEADS
    ctx_blocks = lax.axis_size("ctx")
    ctx_place = lax.axis_index("ctx")
    owners = ctx_blocks * lax.axis_size("dp")
    own_place = lax.axis_index("dp") * ctx_blocks + ctx_place
    doc_most = min(DOC_CAP, length * ctx_blocks // 4)
    reach_blocks = (doc_most - 2 + length) // length
    key_window = (reach_blocks + 1) * length
    score_scale = 1.0 / math.sqrt(HEAD)
    order = owner_order()
    grad_branch = cotangent[0]

    qkv_both = jnp.stack([qkv_weight, pair_swap(qkv_weight)])
    out_weight = after(out_weight, qkv_both)
    out_both = jnp.stack([out_weight, pair_swap(out_weight)])
    w_qkv, qkv_last = gather_rows(qkv_both, order)
    small = jnp.concatenate([qkv_bias, norm_one, norm_two])
    spread = jnp.where(
        (jnp.arange(owners, dtype=jnp.int32) == own_place)[:, None], small[None, :], 0
    ).astype(jnp.bfloat16)
    spread = sum_all(spread)
    bias_size, gain_size = qkv_bias.shape[0], norm_one.shape[0]
    bias = spread[:, :bias_size].reshape(-1).astype(jnp.float32)
    gain_one = spread[:, bias_size : bias_size + gain_size].reshape(-1).astype(jnp.float32)
    gain_two = spread[:, bias_size + gain_size :].reshape(-1).astype(jnp.float32)
    w_out, out_last = gather_rows(after(out_both, qkv_last), order)
    cot_pieces = ring_gather(after(grad_branch, out_last))

    own_rows = after(
        jnp.concatenate([jnp.transpose(gate_up, (1, 0, 2)), down_weight[None]]), out_both
    )
    pair_rows = pair_swap(own_rows)

    scale_one = lax.rsqrt(jnp.mean(tok_rows * tok_rows, axis=-1, keepdims=True) + EPSILON)
    normed_one = tok_rows * scale_one
    act_one = (normed_one * gain_one).astype(jnp.bfloat16)
    qkv_all = jnp.dot(act_one, w_qkv, preferred_element_type=jnp.float32) + bias
    cosine, sine_vals = rope_tables(positions[0])
    query_rot = rotate(
        qkv_all[:, :query_width].reshape(length, HEADS, HEAD), cosine, sine_vals
    ).astype(jnp.bfloat16)
    key_rot = rotate(
        qkv_all[:, query_width : query_width + key_width].reshape(length, KV_HEADS, HEAD),
        cosine,
        sine_vals,
    ).astype(jnp.bfloat16)
    value_own = (
        qkv_all[:, query_width + key_width :].reshape(length, KV_HEADS, HEAD).astype(jnp.bfloat16)
    )
    key_val = jnp.stack([jnp.transpose(key_rot, (1, 0, 2)), jnp.transpose(value_own, (1, 0, 2))])
    window_kv = [key_val]
    for distance in range(1, reach_blocks + 1):
        window_kv.insert(0, from_behind(key_val, distance))
    keys_heads = jnp.concatenate([block[0] for block in window_kv], axis=1)
    values_heads = jnp.concatenate([block[1] for block in window_kv], axis=1)
    key_index = (ctx_place - reach_blocks) * length + jnp.arange(key_window, dtype=jnp.int32)
    query_index = ctx_place * length + jnp.arange(length, dtype=jnp.int32)
    allowed = (key_index[None, :] >= (query_index - positions[0])[:, None]) & (
        key_index[None, :] <= query_index[:, None]
    )
    query_heads = jnp.transpose(query_rot, (1, 0, 2)).reshape(
        KV_HEADS, head_group * length, HEAD
    )
    scores = (
        jnp.einsum("gqd,gkd->gqk", query_heads, keys_heads, preferred_element_type=jnp.float32)
        * score_scale
    ).reshape(KV_HEADS, head_group, length, key_window)
    scores = jnp.where(allowed, scores, -jnp.inf)
    row_top = jnp.max(scores, axis=-1, keepdims=True)
    raised = jnp.exp(scores - row_top)
    row_total = jnp.sum(raised, axis=-1, keepdims=True)
    probs = (raised / row_total).reshape(KV_HEADS, head_group * length, key_window)
    probs_low = probs.astype(jnp.bfloat16)
    attended = jnp.einsum(
        "gqk,gkd->gqd", probs_low, values_heads, preferred_element_type=jnp.float32
    ).astype(jnp.bfloat16)
    attn_rows = jnp.transpose(attended.reshape(HEADS, length, HEAD), (1, 0, 2)).reshape(
        length, query_width
    )
    resid_state = tok_rows + jnp.dot(attn_rows, w_out, preferred_element_type=jnp.float32)
    scale_two = lax.rsqrt(jnp.mean(resid_state * resid_state, axis=-1, keepdims=True) + EPSILON)
    normed_two = resid_state * scale_two
    act_two = (normed_two * gain_two).astype(jnp.bfloat16)

    pair_rows, own_rows = after((pair_rows, own_rows), act_two)
    quarter = [own_rows, pair_rows, core_swap(own_rows), core_swap(pair_rows)]
    w_gate_up = jnp.concatenate([rows[:2] for rows in quarter], axis=1)
    w_down = jnp.concatenate([rows[2] for rows in quarter], axis=0)

    def whole_blocks(pieces):
        return pieces[:-2] + [jnp.concatenate(pieces[-2:])]

    cot_blocks = whole_blocks(cot_pieces)
    group = 2
    acts, cots, hiddens, grads_gu, out_parts, grad_parts = [], [], [], [], [], []

    def mlp_group(act_pieces):
        at = len(acts) * group
        if len(act_pieces) < at + group:
            return []
        act = jnp.concatenate(act_pieces[at : at + group])
        cot = jnp.concatenate(cot_blocks[at : at + group])
        both_vals = jnp.einsum("kcd,td->kct", w_gate_up, act, preferred_element_type=jnp.float32)
        gate_val, up_val = both_vals[0], both_vals[1]
        sigmoid_gate = jax.nn.sigmoid(gate_val)
        silu_gate = gate_val * sigmoid_gate
        hidden = (silu_gate * up_val).astype(jnp.bfloat16)
        grad_hidden = contract(w_down, cot, 1, 1)
        grad_gate = (
            grad_hidden * up_val * sigmoid_gate * (1.0 + gate_val * (1.0 - sigmoid_gate))
        ).astype(jnp.bfloat16)
        grad_up = (grad_hidden * silu_gate).astype(jnp.bfloat16)
        grad_gu = jnp.stack([grad_gate, grad_up])
        grad_parts.append(
            jnp.einsum("kct,kcd->td", grad_gu, w_gate_up, preferred_element_type=jnp.float32)
        )
        out_parts.append(contract(hidden, w_down, 0, 0))
        acts.append(act)
        cots.append(cot)
        hiddens.append(hidden)
        grads_gu.append(grad_gu)
        return [grad_parts[-1], out_parts[-1]]

    act_blocks = whole_blocks(ring_gather(act_two, mlp_group))
    while len(acts) * group < ctx_blocks:
        mlp_group(act_blocks)

    def ring_parts(parts):
        blocks = [part[i * length : (i + 1) * length] for part in parts for i in range(group)]
        return blocks[:-1] + [blocks[-1][: length // 2], blocks[-1][length // 2 :]]

    act_all, cot_all = jnp.concatenate(acts), jnp.concatenate(cots)
    hidden_all = jnp.concatenate(hiddens, axis=1)
    grad_gu_all = jnp.concatenate(grads_gu, axis=2)
    rows_half = hidden_all.shape[0] // 2

    def row_grads(rows):
        gate_up_part = jnp.einsum(
            "kct,td->kcd", grad_gu_all[:, rows], act_all, preferred_element_type=jnp.float32
        )
        return gate_up_part, contract(hidden_all[rows], cot_all, 1, 0)

    theirs_gu, theirs_down = row_grads(slice(rows_half, None))
    mine_gu, mine_down = row_grads(slice(0, rows_half))
    theirs_gu, theirs_down = theirs_gu.astype(jnp.bfloat16), theirs_down.astype(jnp.bfloat16)
    grad_act_two = ring_scatter(
        ring_parts(grad_parts), [[theirs_gu, theirs_down], [mine_gu, mine_down]]
    )
    out_parts = after(tuple(out_parts), grad_act_two)
    mlp_out = ring_scatter(ring_parts(out_parts))
    output = (resid_state + mlp_out).astype(jnp.bfloat16)[None]

    mine_gu = mine_gu + core_swap(theirs_gu).astype(jnp.float32)
    mine_down = mine_down + core_swap(theirs_down).astype(jnp.float32)
    own_size = rows_half // 2
    pair_gu = pair_swap(mine_gu[:, own_size:].astype(jnp.bfloat16))
    pair_down = pair_swap(mine_down[own_size:].astype(jnp.bfloat16))
    gate_up_grad = jnp.transpose(mine_gu[:, :own_size] + pair_gu.astype(jnp.float32), (1, 0, 2))
    down_weight_grad = mine_down[:own_size] + pair_down.astype(jnp.float32)

    gain_two_term = jnp.sum(grad_act_two * normed_two, axis=0)
    grad_state = grad_branch.astype(jnp.float32) + rms_back(
        grad_act_two, normed_two, scale_two, gain_two
    )
    grad_state_b = grad_state.astype(jnp.bfloat16)
    grad_attended = contract(grad_state_b, w_out, 1, 1).astype(jnp.bfloat16)
    grad_heads = jnp.transpose(grad_attended.reshape(length, HEADS, HEAD), (1, 0, 2)).reshape(
        KV_HEADS, head_group * length, HEAD
    )
    grad_probs = jnp.einsum(
        "gqd,gkd->gqk", grad_heads, values_heads, preferred_element_type=jnp.float32
    )
    inner_sum = jnp.sum(probs * grad_probs, axis=-1, keepdims=True)
    grad_scores = (probs * (grad_probs - inner_sum)).astype(jnp.bfloat16)
    grad_keys = (
        jnp.einsum("gqk,gqd->gkd", grad_scores, query_heads, preferred_element_type=jnp.float32)
        * score_scale
    )
    grad_values = jnp.einsum(
        "gqk,gqd->gkd", probs_low, grad_heads, preferred_element_type=jnp.float32
    )
    grad_kv = jnp.stack([grad_keys, grad_values]).reshape(
        2, KV_HEADS, reach_blocks + 1, length, HEAD
    )
    returned = grad_kv[:, :, reach_blocks]
    for distance in range(1, reach_blocks + 1):
        returned = returned + from_behind(
            grad_kv[:, :, reach_blocks - distance].astype(jnp.bfloat16), -distance
        ).astype(jnp.float32)
    grad_query = (
        jnp.einsum("gqk,gkd->gqd", grad_scores, keys_heads, preferred_element_type=jnp.float32)
        * score_scale
    ).reshape(HEADS, length, HEAD)
    grad_query_rows = unrotate(jnp.transpose(grad_query, (1, 0, 2)), cosine, sine_vals).reshape(
        length, query_width
    )
    grad_key_rows = unrotate(jnp.transpose(returned[0], (1, 0, 2)), cosine, sine_vals).reshape(
        length, key_width
    )
    grad_value_rows = jnp.transpose(returned[1], (1, 0, 2)).reshape(length, key_width)
    grad_qkv = jnp.concatenate([grad_query_rows, grad_key_rows, grad_value_rows], axis=-1).astype(
        jnp.bfloat16
    )
    qkv_weight_grad = scatter_rows(act_one, grad_qkv, order)
    out_weight_grad = scatter_rows(attn_rows, grad_state_b, order)
    bias_term = jnp.sum(grad_qkv, axis=0, dtype=jnp.float32)
    grad_act_one = contract(grad_qkv, w_qkv, 1, 1)
    gain_one_term = jnp.sum(grad_act_one * normed_one, axis=0)
    input_grad = (grad_state + rms_back(grad_act_one, normed_one, scale_one, gain_one)).astype(
        jnp.bfloat16
    )[None]
    terms = jnp.concatenate(
        [term.reshape(owners, -1) for term in (bias_term, gain_one_term, gain_two_term)], axis=1
    )
    terms = lax.dynamic_index_in_dim(sum_all(terms), own_place, 0, keepdims=False)
    return (
        output,
        input_grad,
        qkv_weight_grad,
        terms[:bias_size],
        out_weight_grad,
        terms[bias_size : bias_size + gain_size],
        terms[bias_size + gain_size :],
        gate_up_grad,
        down_weight_grad,
    )


def solution(mesh):
    placed = (
        P("dp", "ctx", None),
        P("dp", "ctx"),
        P("dp", "ctx"),
        P(("dp", "ctx"), None),
        P(("dp", "ctx")),
        P(("dp", "ctx"), None),
        P(("dp", "ctx")),
        P(("dp", "ctx")),
        P(("dp", "ctx"), None, None),
        P(("dp", "ctx"), None),
        P("dp", "ctx", None),
    )
    return jax.shard_map(
        shards,
        mesh=mesh,
        in_specs=placed,
        out_specs=(
            P("dp", "ctx", None),
            P("dp", "ctx", None),
            P(("dp", "ctx"), None),
            P(("dp", "ctx")),
            P(("dp", "ctx"), None),
            P(("dp", "ctx")),
            P(("dp", "ctx")),
            P(("dp", "ctx"), None, None),
            P(("dp", "ctx"), None),
        ),
        check_vma=False,
    )
```
